32 devices in a mesh: groups: 2 (over y), prow: 4 (over x, core), pcol: 4 (over z).
Axes of the slice: x: 2, y: 2, z: 4, core: 2. Of those that a mesh axis runs over, the one named last changes fastest.
Arguments:
- anc_inverse: float32 [4096, 2048], P(('groups', 'prow'), 'pcol'), parts along dimension 0
- anc_factor: float32 [8, 2048, 256], P('groups', ('prow', 'pcol')), parts along dimension 0, may hold values from -0.0625 to 0.0625
- win_factor: float32 [12, 256, 256], P('groups'), parts along dimension 0, may hold values from -0.1875 to 0.1875
- diag_inverse: float32 [8, 256, 256], P('groups'), parts along dimension 0
- first_reader: int32 [32], P('groups'), parts along dimension 0, may hold values from 0 to 4
Outputs:
- anc_panels: float32 [8, 2048, 256], P('groups', ('prow', 'pcol')), parts along dimension 0
- window_inverse: float32 [8, 4, 256, 256], P('groups'), parts along dimension 0
The draws below stay inside these ranges and needn't reach their ends.
There are 2 independent parts, one for each index of `groups`. The reference program is written for one: setup_inputs(seed, part) draws one part's arguments, and reference() takes and returns one part's arrays. A program takes and returns all parts, laid end to end along the dimension named above; each array names one. Nothing has to cross between parts.
Inputs may be any that keep to these rules, and one draw needn't show every extreme that they name: Ancestor block b belongs to the pattern of supernode k exactly when first_reader[b] <= k; the value 4 puts it in no pattern, so patterns grow with k. Within each part, anc_inverse is symmetric: anc_inverse[r, s] = anc_inverse[s, r].
All inputs are finite; a program needn't handle non-finite values.
Results may differ from the reference program's by a relative error of at most 0.0003.
Values sent between devices are 32-bit elements; how exact they have to be, the bound alone decides.
A program may use at most 64 MiB of HBM per device.

```python
import math
import jax
import jax.numpy as jnp
from jax import lax

W = 256
K = 4
BLK = 128
S = 2048
SB = 16
PAIRS = 6


def draw_anc_inverse(key, part):
    key_noise, key_scale, key_diag = jax.random.split(key, 3)
    noise = jax.random.normal(key_noise, (S, S), jnp.float32)
    scales = jnp.exp(jax.random.uniform(key_scale, (S,), jnp.float32, 0.0, math.log(10.0)))
    symmetric = (noise + noise.T) * (0.5 / math.sqrt(S))
    diagonal = jax.random.uniform(key_diag, (S,), jnp.float32, 1.0, 4.0)
    sides = jnp.sqrt(scales)
    return symmetric * sides[:, None] * sides[None, :] + jnp.diag(diagonal * scales)


def draw_diag_inverse(key, part):
    key_lower, key_diag = jax.random.split(key, 2)
    lower = jax.random.normal(key_lower, (K, W, W), jnp.float32) * (0.6 / math.sqrt(W))
    diagonal = jax.random.uniform(key_diag, (K, W), jnp.float32, 0.5, 1.5)
    identity = jnp.eye(W, dtype=jnp.float32)
    return jnp.tril(lower, -1) + identity[None, :, :] * diagonal[:, :, None]


def set_ends(result, key, least, largest):
    longest = result.shape.index(max(result.shape))
    spots = []
    for shift in (0, 1):
        where = [jax.random.randint(jax.random.fold_in(key, axis), (), 0, length) for axis, length in enumerate(result.shape)]
        where[longest] = (where[longest] + shift) % result.shape[longest]
        spots.append(tuple(where))
    return result.at[spots[0]].set(least).at[spots[1]].set(largest)


def level_of(own_key, shape, cuts, least, top_value):
    loudness, own = 1.0, jax.random.fold_in(own_key, 6)
    for axis_at, parts in cuts:
        draws = jnp.exp(jax.random.uniform(jax.random.fold_in(own, axis_at), (parts,), jnp.float32, least / len(cuts), top_value / len(cuts)))
        loudness = loudness * jnp.repeat(draws, shape[axis_at] // parts).reshape([-1 if axis == axis_at else 1 for axis in range(len(shape))])
    return loudness


def centred(own_key, extent, spread, limit, cuts=(), kind=jnp.bfloat16):
    drawn = spread * jax.random.normal(own_key, extent, jnp.float32)
    if cuts:
        drawn = drawn * level_of(own_key, extent, cuts, -0.22, 0.18)
    return jnp.clip(drawn, -limit, limit).astype(kind)


def setup_inputs(seed: int = 0, part: int = 0) -> dict:
    arg_keys = jax.random.split(jax.random.key(seed), 6)
    part_splits = jax.random.split(jax.random.fold_in(arg_keys[5], part), 6)
    anc_inverse = draw_anc_inverse(jax.random.fold_in(jax.random.fold_in(arg_keys[5], part), 71), part)
    anc_factor = centred(part_splits[1], (K, S, W), (4 * S) ** -0.5, 0.0625, ((1, 16),), jnp.float32)
    win_factor = centred(part_splits[2], (PAIRS, W, W), (K * W) ** -0.5, 0.1875, (), jnp.float32)
    diag_inverse = draw_diag_inverse(jax.random.fold_in(jax.random.fold_in(arg_keys[5], part), 71), part)
    first_reader = set_ends(jax.random.randint(part_splits[4], (SB,), 0, K + 1), jax.random.fold_in(part_splits[4], 1), 0, K).astype(jnp.int32)
    return dict(anc_inverse=anc_inverse, anc_factor=anc_factor, win_factor=win_factor, diag_inverse=diag_inverse, first_reader=first_reader)


def reference(anc_inverse, anc_factor, win_factor, diag_inverse, first_reader):
    highest = lax.Precision.HIGHEST
    block_of = jnp.arange(S, dtype=jnp.int32) // BLK
    readers = first_reader[block_of]
    panels = [None] * K
    blocks = [[None] * K for column in range(K)]
    for node in reversed(range(K)):
        row_mask = (readers <= node).astype(jnp.float32)[:, None]
        linv = diag_inverse[node]
        later = list(range(node + 1, K))
        lower_u = jnp.dot(anc_factor[node], linv, precision=highest) * row_mask
        upper_u = {}
        for other in later:
            upper_u[other] = jnp.dot(win_factor[other * (other - 1) // 2 + node], linv, precision=highest)
        full_x = jnp.dot(anc_inverse, lower_u, precision=highest)
        for other in later:
            full_x = full_x + jnp.dot(panels[other], upper_u[other], precision=highest)
        cross = {}
        for other in later:
            term = jnp.dot(panels[other].T, lower_u, precision=highest)
            for second in later:
                term = term + jnp.dot(blocks[other][second], upper_u[second], precision=highest)
            cross[other] = term
        panels[node] = -full_x * row_mask
        own = jnp.dot(linv.T, linv, precision=highest) + jnp.dot(lower_u.T, full_x, precision=highest)
        for other in later:
            own = own + jnp.dot(upper_u[other].T, cross[other], precision=highest)
        blocks[node][node] = own
        for other in later:
            blocks[other][node] = -cross[other]
            blocks[node][other] = -cross[other].T
    anc_panels = jnp.stack(panels)
    window_inverse = jnp.stack([jnp.stack(blocks[row_at]) for row_at in range(K)])
    return anc_panels, window_inverse
```

```python
import functools

import jax
import jax.numpy as jnp
from jax import lax
from jax.experimental import pallas as pl
from jax.experimental.pallas import tpu as pltpu
from jax.sharding import PartitionSpec as P

BLK = 128
PIECES = 4
MESH = pl.DeviceIdType.MESH


def split(x):
    high = x.astype(jnp.bfloat16)
    return high, (x - high.astype(jnp.float32)).astype(jnp.bfloat16)


def product(a, b):
    dot = functools.partial(jnp.dot, preferred_element_type=jnp.float32)
    return dot(a[0], b[0]) + (dot(a[0], b[1]) + dot(a[1], b[0]))


def matmul(a, b):
    return product(split(a), split(b))


def pair_at(first, second):
    return second * (second + 1) // 2 + first


def kernel(
    n_prow, n_pcol, readers_ref, a_ref, f_ref, win_ref, diag_ref, panels_ref, z_ref,
    v_ref, whole_ref, part_ref, inbox_ref, g1_send, g1_recv, g2_send, g2_recv, rs_send, rs_recv,
):
    count, fine, width = f_ref.shape
    per_column = n_prow // n_pcol
    step = n_prow // PIECES
    quarter = fine // PIECES
    p = lax.axis_index("prow")
    z = lax.axis_index("pcol")
    order = list(reversed(range(count)))

    barrier = pltpu.get_barrier_semaphore()

    def greet(at, carry):
        row, col = at // n_pcol, at % n_pcol

        @pl.when(at != p * n_pcol + z)
        def _():
            pl.semaphore_signal(barrier, inc=1, device_id={"prow": row, "pcol": col}, device_id_type=MESH)

        return carry

    lax.fori_loop(0, n_prow * n_pcol, greet, 0)

    reader = readers_ref[(p * n_pcol + z) * fine // BLK]
    masks = [jnp.where(reader <= node, 1.0, 0.0).astype(jnp.float32) for node in range(count)]

    def local_v(node):
        total = f_ref[node] * masks[node]
        for other in range(node + 1, count):
            total = total - matmul(v_ref[other], win_ref[other * (other - 1) // 2 + node])
        v_ref[node] = matmul(total, diag_ref[node])

    source = (p % per_column) * n_pcol + z
    column = p // per_column

    def g1_copy(node, q):
        return pltpu.make_async_remote_copy(
            src_ref=v_ref.at[node, pl.ds(q * quarter, quarter)],
            dst_ref=whole_ref.at[node, source, q],
            send_sem=g1_send.at[node, q],
            recv_sem=g1_recv.at[node],
            device_id={"prow": q * step, "pcol": column},
            device_id_type=MESH,
        )

    def g1_start(node):
        for q in range(PIECES):
            mine = jnp.logical_and(p == q * step, z == column)

            @pl.when(mine)
            def _():
                pltpu.make_async_copy(
                    v_ref.at[node, pl.ds(q * quarter, quarter)],
                    whole_ref.at[node, source, q],
                    g1_recv.at[node],
                ).start()

            @pl.when(jnp.logical_not(mine))
            def _():
                g1_copy(node, q).start()

    def g1_finish(node):
        for q in range(PIECES):
            mine = jnp.logical_and(p == q * step, z == column)

            @pl.when(jnp.logical_not(mine))
            def _():
                g1_copy(node, q).wait_send()

    def g2_copy(node, q, row):
        return pltpu.make_async_remote_copy(
            src_ref=whole_ref.at[node, :, q],
            dst_ref=whole_ref.at[node, :, q],
            send_sem=g2_send.at[node, row],
            recv_sem=g2_recv.at[node, q],
            device_id={"prow": row, "pcol": z},
            device_id_type=MESH,
        )

    def g2_start(node):
        for q in range(PIECES):
            @pl.when(p == q * step)
            def _():
                held = whole_ref.at[node, :, q]
                pltpu.make_async_copy(held, held, g1_recv.at[node]).wait()
                for row in range(n_prow):
                    if row != q * step:
                        g2_copy(node, q, row).start()

    def g2_wait(node):
        for q in range(PIECES):
            @pl.when(p != q * step)
            def _():
                g2_copy(node, q, 0).wait_recv()

    def g2_finish(node):
        for q in range(PIECES):
            @pl.when(p == q * step)
            def _():
                for row in range(n_prow):
                    if row != q * step:
                        g2_copy(node, q, row).wait_send()

    def rs_copy(node, side, dest):
        return pltpu.make_async_remote_copy(
            src_ref=part_ref.at[node, dest],
            dst_ref=inbox_ref.at[node, side, dest],
            send_sem=rs_send.at[node, dest],
            recv_sem=rs_recv.at[node, side, dest],
            device_id={"prow": p, "pcol": z + 1 if side == 0 else z - 1},
            device_id_type=MESH,
        )

    def rs_steps(node, relayed):
        for far in range(1, n_pcol):
            for side in (0, 1):
                dest = n_pcol - far if side == 0 else far - 1
                first = z == (0 if side == 0 else n_pcol - 1)
                before = z < dest if side == 0 else z > dest
                if relayed:
                    @pl.when(jnp.logical_and(before, jnp.logical_not(first)))
                    def _():
                        rs_copy(node, side, dest).wait_recv()
                        part_ref[node, dest] += inbox_ref[node, side, dest]
                        rs_copy(node, side, dest).start()
                else:
                    @pl.when(jnp.logical_and(before, first))
                    def _():
                        rs_copy(node, side, dest).start()

    def rs_end(node):
        for dest in range(n_pcol):
            @pl.when(z == dest)
            def _():
                total = part_ref[node, dest]
                if dest > 0:
                    rs_copy(node, 0, dest).wait_recv()
                    total = total + inbox_ref[node, 0, dest]
                if dest < n_pcol - 1:
                    rs_copy(node, 1, dest).wait_recv()
                    total = total + inbox_ref[node, 1, dest]
                part_ref[node, dest] = total
                panels_ref[node] = -total * masks[node]

    def rs_finish(node):
        for dest in range(n_pcol):
            @pl.when(z != dest)
            def _():
                rs_copy(node, 0, dest).wait_send()

    a_split = []

    def multiply(node):
        rows = a_ref.shape[0]
        gathered = whole_ref[node].reshape(a_ref.shape[1], width)
        result = product(a_split[0], split(gathered))
        part_ref[node] = result.reshape(n_pcol, fine, width)

    vt_split = {}

    def window_part(node):
        x = split(-panels_x(node))
        for other in range(node + 1):
            z_ref[pair_at(other, node)] = product(vt_split[other], x)

    def panels_x(node):
        return -part_ref[node, z]

    local_v(order[0])
    pl.semaphore_wait(barrier, n_prow * n_pcol - 1)
    g1_start(order[0])
    for node in order[1:]:
        local_v(node)
        g1_start(node)
    a_split.append(split(a_ref[...]))
    for node in range(count):
        vt_split[node] = split(v_ref[node].T)
    g2_start(order[0])
    for at, node in enumerate(order):
        if at + 1 < count:
            g2_start(order[at + 1])
        g2_wait(node)
        multiply(node)
        rs_steps(node, False)
        if at >= 1:
            rs_steps(order[at - 1], True)
        if at >= 2:
            rs_end(order[at - 2])
            window_part(order[at - 2])
    rs_steps(order[-1], True)
    for node in order[max(count - 2, 0):]:
        rs_end(node)
        window_part(node)
    for node in order:
        g1_finish(node)
        g2_finish(node)
        rs_finish(node)


def sweep(n_prow, n_pcol, readers, anc_inverse, anc_factor, win_factor, diag_inverse):
    count, fine, width = anc_factor.shape
    pairs = count * (count + 1) // 2
    sources = n_prow // n_pcol * n_pcol
    vmem = pl.BlockSpec(memory_space=pltpu.VMEM)
    return pl.pallas_call(
        functools.partial(kernel, n_prow, n_pcol),
        out_shape=(
            jax.ShapeDtypeStruct((count, fine, width), jnp.float32),
            jax.ShapeDtypeStruct((pairs, width, width), jnp.float32),
        ),
        in_specs=[pl.BlockSpec(memory_space=pltpu.SMEM)] + [vmem] * 4,
        out_specs=(vmem, vmem),
        scratch_shapes=[
            pltpu.VMEM((count, fine, width), jnp.float32),
            pltpu.VMEM((count, sources, PIECES, fine // PIECES, width), jnp.float32),
            pltpu.VMEM((count, n_pcol, fine, width), jnp.float32),
            pltpu.VMEM((count, 2, n_pcol, fine, width), jnp.float32),
            pltpu.SemaphoreType.DMA((count, PIECES)),
            pltpu.SemaphoreType.DMA((count,)),
            pltpu.SemaphoreType.DMA((count, n_prow)),
            pltpu.SemaphoreType.DMA((count, PIECES)),
            pltpu.SemaphoreType.DMA((count, n_pcol)),
            pltpu.SemaphoreType.DMA((count, 2, n_pcol)),
        ],
        compiler_params=pltpu.CompilerParams(
            collective_id=0, has_side_effects=True, vmem_limit_bytes=48 * 2**20
        ),
    )(readers, anc_inverse, anc_factor, win_factor, diag_inverse)


def window_own(win_factor, diag_inverse):
    dot = functools.partial(jnp.dot, precision=lax.Precision.HIGH)
    count, width, _ = diag_inverse.shape
    columns = []
    for node in range(count):
        column = [jnp.zeros((width, width), jnp.float32)] * node + [diag_inverse[node]]
        for row in range(node + 1, count):
            total = sum(dot(win_factor[row * (row - 1) // 2 + at], column[at]) for at in range(node, row))
            column.append(-dot(diag_inverse[row], total))
        columns.append(jnp.concatenate(column, axis=0))
    whole = jnp.concatenate(columns, axis=1)
    return dot(whole.T, whole)


def per_device(anc_inverse, anc_factor, win_factor, diag_inverse, first_reader):
    n_prow = lax.axis_size("prow")
    n_pcol = lax.axis_size("pcol")
    count, _, width = anc_factor.shape
    panels, partial = sweep(
        n_prow, n_pcol, first_reader, anc_inverse, anc_factor, win_factor, diag_inverse
    )
    own = window_own(win_factor, diag_inverse)
    summed = lax.psum(partial, ("prow", "pcol"))
    own = own.reshape(count, width, count, width).transpose(0, 2, 1, 3)
    cross = jnp.stack([
        jnp.stack([
            summed[pair_at(row, col)] if row <= col else summed[pair_at(col, row)].T
            for col in range(count)
        ])
        for row in range(count)
    ])
    return panels, own + cross


def solution(mesh):
    return jax.shard_map(
        per_device,
        mesh=mesh,
        in_specs=(
            P(("groups", "prow"), "pcol"),
            P("groups", ("prow", "pcol"), None),
            P("groups", None, None),
            P("groups", None, None),
            P("groups"),
        ),
        out_specs=(P("groups", ("prow", "pcol"), None), P("groups", None, None, None)),
        check_vma=False,
    )
```

```python
import functools

import jax
import jax.numpy as jnp
from jax import lax
from jax.experimental import pallas as pl
from jax.experimental.pallas import tpu as pltpu
from jax.sharding import PartitionSpec as P

BLK = 128
PIECES = 4
MESH = pl.DeviceIdType.MESH


def split(x):
    high = x.astype(jnp.bfloat16)
    return high, (x - high.astype(jnp.float32)).astype(jnp.bfloat16)


def product(a, b):
    dot = functools.partial(jnp.dot, preferred_element_type=jnp.float32)
    return dot(a[0], b[0]) + (dot(a[0], b[1]) + dot(a[1], b[0]))


def matmul(a, b):
    return product(split(a), split(b))


def pair_at(first, second):
    return second * (second + 1) // 2 + first


def kernel(
    n_prow, n_pcol, readers_ref, a_hbm, f_hbm, win_hbm, diag_hbm, panels_ref, window_ref,
    a_ref, f_ref, win_ref, diag_ref, v_ref, whole_ref, part_ref, inbox_ref, sum_ref, final_ref,
    line_ref, load_sem, g1_send, g1_recv, g2_send, g2_recv, rs_send, rs_recv,
    half_send, half_recv, line_send, line_recv, back_send, back_recv, whole_send, whole_recv, *half_refs,
):
    loads = [
        pltpu.make_async_copy(source, target, load_sem.at[at])
        for at, (source, target) in enumerate(
            [(f_hbm, f_ref), (diag_hbm, diag_ref), (win_hbm, win_ref), (a_hbm, a_ref)]
        )
    ]
    for load in loads:
        load.start()
    count, fine, width = f_ref.shape
    per_column = n_prow // n_pcol
    step = n_prow // PIECES
    quarter = fine // PIECES
    p = lax.axis_index("prow")
    z = lax.axis_index("pcol")
    order = list(reversed(range(count)))

    barrier = pltpu.get_barrier_semaphore()

    def greet(at, carry):
        row, col = at // n_pcol, at % n_pcol

        @pl.when(at != p * n_pcol + z)
        def _():
            pl.semaphore_signal(barrier, inc=1, device_id={"prow": row, "pcol": col}, device_id_type=MESH)

        return carry

    lax.fori_loop(0, n_prow * n_pcol, greet, 0)

    reader = readers_ref[(p * n_pcol + z) * fine // BLK]
    masks = [jnp.where(reader <= node, 1.0, 0.0).astype(jnp.float32) for node in range(count)]

    share = v_ref.shape[1] - fine
    unit_row = lax.broadcasted_iota(jnp.int32, (share, width), 0) + (p * n_pcol + z) * share
    unit_col = lax.broadcasted_iota(jnp.int32, (share, width), 1)

    def local_v(node):
        units = jnp.where(unit_row == unit_col + node * width, 1.0, 0.0).astype(jnp.float32)
        total = jnp.concatenate([f_ref[node] * masks[node], units], axis=0)
        for other in range(node + 1, count):
            total = total - matmul(v_ref[other], win_ref[other * (other - 1) // 2 + node])
        v_ref[node] = matmul(total, diag_ref[node])

    source = (p % per_column) * n_pcol + z
    column = p // per_column

    def g1_copy(node, q):
        return pltpu.make_async_remote_copy(
            src_ref=v_ref.at[node, pl.ds(q * quarter, quarter)],
            dst_ref=whole_ref.at[node, source, q],
            send_sem=g1_send.at[node, q],
            recv_sem=g1_recv.at[node],
            device_id={"prow": q * step, "pcol": column},
            device_id_type=MESH,
        )

    def g1_start(node):
        for q in range(PIECES):
            mine = jnp.logical_and(p == q * step, z == column)

            @pl.when(mine)
            def _():
                pltpu.make_async_copy(
                    v_ref.at[node, pl.ds(q * quarter, quarter)],
                    whole_ref.at[node, source, q],
                    g1_recv.at[node],
                ).start()

            @pl.when(jnp.logical_not(mine))
            def _():
                g1_copy(node, q).start()

    def g1_finish(node):
        for q in range(PIECES):
            mine = jnp.logical_and(p == q * step, z == column)

            @pl.when(jnp.logical_not(mine))
            def _():
                g1_copy(node, q).wait_send()

    def g2_copy(node, q, row):
        return pltpu.make_async_remote_copy(
            src_ref=whole_ref.at[node, :, q],
            dst_ref=whole_ref.at[node, :, q],
            send_sem=g2_send.at[node, row],
            recv_sem=g2_recv.at[node, q],
            device_id={"prow": row, "pcol": z},
            device_id_type=MESH,
        )

    def g2_start(node):
        for q in range(PIECES):
            @pl.when(p == q * step)
            def _():
                held = whole_ref.at[node, :, q]
                pltpu.make_async_copy(held, held, g1_recv.at[node]).wait()
                for row in range(n_prow):
                    if row != q * step:
                        g2_copy(node, q, row).start()

    def g2_wait(node):
        for q in range(PIECES):
            @pl.when(p != q * step)
            def _():
                g2_copy(node, q, 0).wait_recv()

    def g2_finish(node):
        for q in range(PIECES):
            @pl.when(p == q * step)
            def _():
                for row in range(n_prow):
                    if row != q * step:
                        g2_copy(node, q, row).wait_send()

    def rs_copy(node, side, dest):
        return pltpu.make_async_remote_copy(
            src_ref=part_ref.at[node, dest],
            dst_ref=inbox_ref.at[node, side, dest],
            send_sem=rs_send.at[node, dest],
            recv_sem=rs_recv.at[node, side, dest],
            device_id={"prow": p, "pcol": z + 1 if side == 0 else z - 1},
            device_id_type=MESH,
        )

    def rs_steps(node, relayed):
        for far in range(1, n_pcol):
            for side in (0, 1):
                dest = n_pcol - far if side == 0 else far - 1
                first = z == (0 if side == 0 else n_pcol - 1)
                before = z < dest if side == 0 else z > dest
                if relayed:
                    @pl.when(jnp.logical_and(before, jnp.logical_not(first)))
                    def _():
                        rs_copy(node, side, dest).wait_recv()
                        part_ref[node, dest] += inbox_ref[node, side, dest]
                        rs_copy(node, side, dest).start()
                else:
                    @pl.when(jnp.logical_and(before, first))
                    def _():
                        rs_copy(node, side, dest).start()

    def rs_end(node):
        for dest in range(n_pcol):
            @pl.when(z == dest)
            def _():
                total = part_ref[node, dest]
                if dest > 0:
                    rs_copy(node, 0, dest).wait_recv()
                    total = total + inbox_ref[node, 0, dest]
                if dest < n_pcol - 1:
                    rs_copy(node, 1, dest).wait_recv()
                    total = total + inbox_ref[node, 1, dest]
                part_ref[node, dest] = total
                panels_ref[node] = -total * masks[node]

    def rs_finish(node):
        for dest in range(n_pcol):
            @pl.when(z != dest)
            def _():
                rs_copy(node, 0, dest).wait_send()

    a_split = []

    def multiply(node):
        rows = a_ref.shape[0]
        gathered = whole_ref[node].reshape(a_ref.shape[1], width)
        result = product(a_split[0], split(gathered))
        part_ref[node] = result.reshape(n_pcol, fine, width)

    vt_split = {}

    def window_part(node):
        x = split(jnp.concatenate([part_ref[node, z], v_ref[node, pl.ds(fine, share)]], axis=0))
        for other in range(node + 1):
            sum_ref[pair_at(other, node)] = product(vt_split[other], x)

    bits = len(half_refs)
    starts = [0]
    for bit in range(bits):
        starts.append(starts[bit] + (p // 2**bit) % 2 * (width // 2 ** (bit + 1)))
    region = width // n_prow
    full = region // n_pcol % 8 != 0
    piece = region if full else region // n_pcol

    def blocks(node):
        return pl.ds(pair_at(0, node), node + 1)

    def rows(start, size):
        return pl.ds(pl.multiple_of(start, 8), size)

    def partner(bit):
        return {"prow": p + (1 - (p // 2**bit) % 2 * 2) * 2**bit, "pcol": z}

    def half_copy(node, bit):
        half = width // 2 ** (bit + 1)
        away = starts[bit] + (1 - (p // 2**bit) % 2) * half
        return pltpu.make_async_remote_copy(
            src_ref=sum_ref.at[blocks(node), rows(away, half)],
            dst_ref=half_refs[bit].at[blocks(node)],
            send_sem=half_send.at[node, bit],
            recv_sem=half_recv.at[node, bit],
            device_id=partner(bit),
            device_id_type=MESH,
        )

    def half_end(node, bit):
        half_copy(node, bit).wait_recv()
        mine = rows(starts[bit + 1], width // 2 ** (bit + 1))
        sum_ref[blocks(node), mine] += half_refs[bit][blocks(node)]

    def piece_rows(dest):
        return rows(starts[bits] if full else starts[bits] + dest * piece, piece)

    def line_copy(node, dest, source):
        return pltpu.make_async_remote_copy(
            src_ref=sum_ref.at[blocks(node), piece_rows(dest)],
            dst_ref=line_ref.at[source, blocks(node)],
            send_sem=line_send.at[node, dest],
            recv_sem=line_recv.at[node, source],
            device_id={"prow": p, "pcol": dest},
            device_id_type=MESH,
        )

    def back_copy(node, dest, source):
        return pltpu.make_async_remote_copy(
            src_ref=final_ref.at[blocks(node), piece_rows(source)],
            dst_ref=final_ref.at[blocks(node), piece_rows(source)],
            send_sem=back_send.at[node, dest],
            recv_sem=back_recv.at[node, source],
            device_id={"prow": p, "pcol": dest},
            device_id_type=MESH,
        )

    def others(run):
        for at in range(n_pcol):
            @pl.when(z != at)
            def _():
                run(at)

    def line_end(node):
        def add(source):
            line_copy(node, z, source).wait_recv()
            sum_ref[blocks(node), piece_rows(z)] += line_ref[source, blocks(node)]

        if full:
            sum_at = jnp.zeros((node + 1, piece, width), jnp.float32)
            line_ref[z, blocks(node)] = sum_ref[blocks(node), piece_rows(z)]
            others(lambda source: line_copy(node, z, source).wait_recv())
            for source in range(n_pcol):
                sum_at = sum_at + line_ref[source, blocks(node)]
            final_ref[blocks(node), piece_rows(z)] = sum_at
        else:
            others(add)
            final_ref[blocks(node), piece_rows(z)] = sum_ref[blocks(node), piece_rows(z)]

    def whole_copy(node, bit, start):
        part = rows(start, width // 2 ** (bit + 1))
        return pltpu.make_async_remote_copy(
            src_ref=final_ref.at[blocks(node), part],
            dst_ref=final_ref.at[blocks(node), part],
            send_sem=whole_send.at[node, bit],
            recv_sem=whole_recv.at[node, bit],
            device_id=partner(bit),
            device_id_type=MESH,
        )

    def whole_start(node, bit):
        whole_copy(node, bit, starts[bit + 1]).start()

    def whole_end(node, bit):
        whole_copy(node, bit, starts[bit + 1]).wait_recv()

    def write(node):
        for other in range(node + 1):
            block = final_ref[pair_at(other, node)]
            window_ref[other, node] = block
            if other < node:
                window_ref[node, other] = block.T

    def stage(node, at):
        if at == 0:
            g2_wait(node)
            multiply(node)
            rs_steps(node, False)
        elif at == 1:
            rs_steps(node, True)
        elif at == 2:
            rs_end(node)
            window_part(node)
            half_copy(node, 0).start()
        elif at < 3 + bits:
            bit = at - 3
            half_end(node, bit)
            if bit + 1 < bits:
                half_copy(node, bit + 1).start()
            else:
                others(lambda dest: line_copy(node, dest, z).start())
        elif at == 3 + bits:
            line_end(node)
            if not full:
                others(lambda dest: back_copy(node, dest, z).start())
        elif at == 4 + bits:
            if not full:
                others(lambda source: back_copy(node, z, source).wait_recv())
            whole_start(node, bits - 1)
        else:
            bit = 2 * bits + 4 - at
            whole_end(node, bit)
            if bit > 0:
                whole_start(node, bit - 1)
            else:
                write(node)

    loads[0].wait()
    loads[1].wait()
    local_v(order[0])
    pl.semaphore_wait(barrier, n_prow * n_pcol - 1)
    g1_start(order[0])
    loads[2].wait()
    for node in order[1:]:
        local_v(node)
        g1_start(node)
    loads[3].wait()
    a_split.append(split(a_ref[...]))
    for node in range(count):
        vt_split[node] = split(v_ref[node].T)
    g2_start(order[0])
    last = 5 + 2 * bits
    for turn in range(count + last - 1):
        if turn + 1 < count:
            g2_start(order[turn + 1])
        for at in range(last):
            if 0 <= turn - at < count:
                stage(order[turn - at], at)
    for node in order:
        g1_finish(node)
        g2_finish(node)
        rs_finish(node)
        for bit in range(bits):
            half_copy(node, bit).wait_send()
            whole_copy(node, bit, starts[bit + 1]).wait_send()
        others(lambda dest: line_copy(node, dest, z).wait_send())
        if not full:
            others(lambda dest: back_copy(node, dest, z).wait_send())


def sweep(n_prow, n_pcol, readers, anc_inverse, anc_factor, win_factor, diag_inverse):
    count, fine, width = anc_factor.shape
    pairs = count * (count + 1) // 2
    sources = n_prow // n_pcol * n_pcol
    share = count * width // (n_prow * n_pcol)
    bits = n_prow.bit_length() - 1
    region = width // n_prow
    piece = region if region // n_pcol % 8 != 0 else region // n_pcol
    vmem = pl.BlockSpec(memory_space=pltpu.VMEM)
    operands = (anc_inverse, anc_factor, win_factor, diag_inverse)
    return pl.pallas_call(
        functools.partial(kernel, n_prow, n_pcol),
        out_shape=(
            jax.ShapeDtypeStruct((count, fine, width), jnp.float32),
            jax.ShapeDtypeStruct((count, count, width, width), jnp.float32),
        ),
        in_specs=[pl.BlockSpec(memory_space=pltpu.SMEM)] + [pl.BlockSpec(memory_space=pltpu.HBM)] * 4,
        out_specs=(vmem, vmem),
        scratch_shapes=[pltpu.VMEM(operand.shape, jnp.float32) for operand in operands]
        + [
            pltpu.VMEM((count, fine + share, width), jnp.float32),
            pltpu.VMEM((count, sources, PIECES, fine // PIECES, width), jnp.float32),
            pltpu.VMEM((count, n_pcol, fine, width), jnp.float32),
            pltpu.VMEM((count, 2, n_pcol, fine, width), jnp.float32),
            pltpu.VMEM((pairs, width, width), jnp.float32),
            pltpu.VMEM((pairs, width, width), jnp.float32),
            pltpu.VMEM((n_pcol, pairs, piece, width), jnp.float32),
            pltpu.SemaphoreType.DMA((len(operands),)),
            pltpu.SemaphoreType.DMA((count, PIECES)),
            pltpu.SemaphoreType.DMA((count,)),
            pltpu.SemaphoreType.DMA((count, n_prow)),
            pltpu.SemaphoreType.DMA((count, PIECES)),
            pltpu.SemaphoreType.DMA((count, n_pcol)),
            pltpu.SemaphoreType.DMA((count, 2, n_pcol)),
            pltpu.SemaphoreType.DMA((count, bits)),
            pltpu.SemaphoreType.DMA((count, bits)),
            pltpu.SemaphoreType.DMA((count, n_pcol)),
            pltpu.SemaphoreType.DMA((count, n_pcol)),
            pltpu.SemaphoreType.DMA((count, n_pcol)),
            pltpu.SemaphoreType.DMA((count, n_pcol)),
            pltpu.SemaphoreType.DMA((count, bits)),
            pltpu.SemaphoreType.DMA((count, bits)),
        ]
        + [pltpu.VMEM((pairs, width // 2 ** (bit + 1), width), jnp.float32) for bit in range(bits)],
        compiler_params=pltpu.CompilerParams(
            collective_id=0, has_side_effects=True, vmem_limit_bytes=56 * 2**20
        ),
    )(readers, *operands)


def per_device(anc_inverse, anc_factor, win_factor, diag_inverse, first_reader):
    n_prow = lax.axis_size("prow")
    n_pcol = lax.axis_size("pcol")
    return sweep(n_prow, n_pcol, first_reader, anc_inverse, anc_factor, win_factor, diag_inverse)


def solution(mesh):
    return jax.shard_map(
        per_device,
        mesh=mesh,
        in_specs=(
            P(("groups", "prow"), "pcol"),
            P("groups", ("prow", "pcol"), None),
            P("groups", None, None),
            P("groups", None, None),
            P("groups"),
        ),
        out_specs=(P("groups", ("prow", "pcol"), None), P("groups", None, None, None)),
        check_vma=False,
    )
```

```python
import functools

import jax
import jax.numpy as jnp
from jax import lax
from jax.experimental import pallas as pl
from jax.experimental.pallas import tpu as pltpu
from jax.sharding import PartitionSpec as P

BLK = 128
PIECES = 4
MESH = pl.DeviceIdType.MESH


def split(x):
    high = x.astype(jnp.bfloat16)
    return high, (x - high.astype(jnp.float32)).astype(jnp.bfloat16)


def product(a, b):
    dot = functools.partial(jnp.dot, preferred_element_type=jnp.float32)
    return dot(a[0], b[0]) + (dot(a[0], b[1]) + dot(a[1], b[0]))


def matmul(a, b):
    return product(split(a), split(b))


def pair_at(first, second):
    return second * (second + 1) // 2 + first


def kernel(
    n_prow, n_pcol, readers_ref, a_hbm, f_hbm, win_hbm, diag_hbm, panels_ref, window_ref,
    a_ref, f_ref, win_ref, diag_ref, v_ref, whole_ref, part_ref, inbox_ref, sum_ref, final_ref,
    line_ref, load_sem, g1_send, g1_recv, g2_send, g2_recv, rs_send, rs_recv,
    half_send, half_recv, line_send, line_recv, back_send, back_recv, whole_send, whole_recv, *half_refs,
):
    loads = [
        pltpu.make_async_copy(source, target, load_sem.at[at])
        for at, (source, target) in enumerate(
            [(f_hbm, f_ref), (diag_hbm, diag_ref), (win_hbm, win_ref), (a_hbm, a_ref)]
        )
    ]
    for load in loads:
        load.start()
    count, fine, width = f_ref.shape
    per_column = n_prow // n_pcol
    step = n_prow // PIECES
    quarter = fine // PIECES
    p = lax.axis_index("prow")
    z = lax.axis_index("pcol")
    order = list(reversed(range(count)))

    barrier = pltpu.get_barrier_semaphore()

    def greet(at, carry):
        row, col = at // n_pcol, at % n_pcol

        @pl.when(at != p * n_pcol + z)
        def _():
            pl.semaphore_signal(barrier, inc=1, device_id={"prow": row, "pcol": col}, device_id_type=MESH)

        return carry

    lax.fori_loop(0, n_prow * n_pcol, greet, 0)

    reader = readers_ref[(p * n_pcol + z) * fine // BLK]
    masks = [jnp.where(reader <= node, 1.0, 0.0).astype(jnp.float32) for node in range(count)]

    share = v_ref.shape[1] - fine
    unit_row = lax.broadcasted_iota(jnp.int32, (share, width), 0) + (p * n_pcol + z) * share
    unit_col = lax.broadcasted_iota(jnp.int32, (share, width), 1)

    def local_v(node):
        units = jnp.where(unit_row == unit_col + node * width, 1.0, 0.0).astype(jnp.float32)
        total = jnp.concatenate([f_ref[node] * masks[node], units], axis=0)
        for other in range(node + 1, count):
            total = total - matmul(v_ref[other], win_ref[other * (other - 1) // 2 + node])
        v_ref[node] = matmul(total, diag_ref[node])

    source = (p % per_column) * n_pcol + z
    column = p // per_column

    def g1_copy(node, q):
        return pltpu.make_async_remote_copy(
            src_ref=v_ref.at[node, pl.ds(q * quarter, quarter)],
            dst_ref=whole_ref.at[node, source, q],
            send_sem=g1_send.at[node, q],
            recv_sem=g1_recv.at[node],
            device_id={"prow": q * step, "pcol": column},
            device_id_type=MESH,
        )

    def g1_start(node):
        for q in range(PIECES):
            mine = jnp.logical_and(p == q * step, z == column)

            @pl.when(mine)
            def _():
                pltpu.make_async_copy(
                    v_ref.at[node, pl.ds(q * quarter, quarter)],
                    whole_ref.at[node, source, q],
                    g1_recv.at[node],
                ).start()

            @pl.when(jnp.logical_not(mine))
            def _():
                g1_copy(node, q).start()

    def g1_finish(node):
        for q in range(PIECES):
            mine = jnp.logical_and(p == q * step, z == column)

            @pl.when(jnp.logical_not(mine))
            def _():
                g1_copy(node, q).wait_send()

    def g2_copy(node, q, row):
        return pltpu.make_async_remote_copy(
            src_ref=whole_ref.at[node, :, q],
            dst_ref=whole_ref.at[node, :, q],
            send_sem=g2_send.at[node, row],
            recv_sem=g2_recv.at[node, q],
            device_id={"prow": row, "pcol": z},
            device_id_type=MESH,
        )

    def g2_start(node):
        for q in range(PIECES):
            @pl.when(p == q * step)
            def _():
                held = whole_ref.at[node, :, q]
                pltpu.make_async_copy(held, held, g1_recv.at[node]).wait()
                for row in range(n_prow):
                    if row != q * step:
                        g2_copy(node, q, row).start()

    def g2_wait(node):
        for q in range(PIECES):
            @pl.when(p != q * step)
            def _():
                g2_copy(node, q, 0).wait_recv()

    def g2_finish(node):
        for q in range(PIECES):
            @pl.when(p == q * step)
            def _():
                for row in range(n_prow):
                    if row != q * step:
                        g2_copy(node, q, row).wait_send()

    def rs_copy(node, side, dest):
        return pltpu.make_async_remote_copy(
            src_ref=part_ref.at[node, dest],
            dst_ref=inbox_ref.at[node, side, dest],
            send_sem=rs_send.at[node, dest],
            recv_sem=rs_recv.at[node, side, dest],
            device_id={"prow": p, "pcol": z + 1 if side == 0 else z - 1},
            device_id_type=MESH,
        )

    def rs_steps(node, relayed):
        for far in range(1, n_pcol):
            for side in (0, 1):
                dest = n_pcol - far if side == 0 else far - 1
                first = z == (0 if side == 0 else n_pcol - 1)
                before = z < dest if side == 0 else z > dest
                if relayed:
                    @pl.when(jnp.logical_and(before, jnp.logical_not(first)))
                    def _():
                        rs_copy(node, side, dest).wait_recv()
                        part_ref[node, dest] += inbox_ref[node, side, dest]
                        rs_copy(node, side, dest).start()
                else:
                    @pl.when(jnp.logical_and(before, first))
                    def _():
                        rs_copy(node, side, dest).start()

    def rs_end(node):
        for dest in range(n_pcol):
            @pl.when(z == dest)
            def _():
                total = part_ref[node, dest]
                if dest > 0:
                    rs_copy(node, 0, dest).wait_recv()
                    total = total + inbox_ref[node, 0, dest]
                if dest < n_pcol - 1:
                    rs_copy(node, 1, dest).wait_recv()
                    total = total + inbox_ref[node, 1, dest]
                part_ref[node, dest] = total
                panels_ref[node] = -total * masks[node]

    def rs_finish(node):
        for dest in range(n_pcol):
            @pl.when(z != dest)
            def _():
                rs_copy(node, 0, dest).wait_send()

    a_split = []

    def multiply(node):
        rows = a_ref.shape[0]
        gathered = whole_ref[node].reshape(a_ref.shape[1], width)
        result = product(a_split[0], split(gathered))
        part_ref[node] = result.reshape(n_pcol, fine, width)

    vt_split = {}

    def window_part(node):
        x = split(jnp.concatenate([part_ref[node, z], v_ref[node, pl.ds(fine, share)]], axis=0))
        for other in range(node + 1):
            sum_ref[pair_at(other, node)] = product(vt_split[other], x)

    bits = len(half_refs)
    starts = [0]
    for bit in range(bits):
        starts.append(starts[bit] + (p // 2**bit) % 2 * (width // 2 ** (bit + 1)))
    region = width // n_prow
    full = region // n_pcol % 8 != 0
    piece = region if full else region // n_pcol

    def blocks(node):
        return pl.ds(pair_at(0, node), node + 1)

    def rows(start, size):
        return pl.ds(pl.multiple_of(start, 8), size)

    def partner(bit):
        return {"prow": p + (1 - (p // 2**bit) % 2 * 2) * 2**bit, "pcol": z}

    def half_copy(node, bit):
        half = width // 2 ** (bit + 1)
        away = starts[bit] + (1 - (p // 2**bit) % 2) * half
        return pltpu.make_async_remote_copy(
            src_ref=sum_ref.at[blocks(node), rows(away, half)],
            dst_ref=half_refs[bit].at[blocks(node)],
            send_sem=half_send.at[node, bit],
            recv_sem=half_recv.at[node, bit],
            device_id=partner(bit),
            device_id_type=MESH,
        )

    def half_end(node, bit):
        half_copy(node, bit).wait_recv()
        mine = rows(starts[bit + 1], width // 2 ** (bit + 1))
        sum_ref[blocks(node), mine] += half_refs[bit][blocks(node)]

    def piece_rows(dest):
        return rows(starts[bits] if full else starts[bits] + dest * piece, piece)

    def line_copy(node, dest, source):
        return pltpu.make_async_remote_copy(
            src_ref=sum_ref.at[blocks(node), piece_rows(dest)],
            dst_ref=line_ref.at[source, blocks(node)],
            send_sem=line_send.at[node, dest],
            recv_sem=line_recv.at[node, source],
            device_id={"prow": p, "pcol": dest},
            device_id_type=MESH,
        )

    def back_copy(node, dest, source):
        return pltpu.make_async_remote_copy(
            src_ref=final_ref.at[blocks(node), piece_rows(source)],
            dst_ref=final_ref.at[blocks(node), piece_rows(source)],
            send_sem=back_send.at[node, dest],
            recv_sem=back_recv.at[node, source],
            device_id={"prow": p, "pcol": dest},
            device_id_type=MESH,
        )

    def others(run):
        for at in range(n_pcol):
            @pl.when(z != at)
            def _():
                run(at)

    def line_end(node):
        def add(source):
            line_copy(node, z, source).wait_recv()
            sum_ref[blocks(node), piece_rows(z)] += line_ref[source, blocks(node)]

        if full:
            sum_at = jnp.zeros((node + 1, piece, width), jnp.float32)
            line_ref[z, blocks(node)] = sum_ref[blocks(node), piece_rows(z)]
            others(lambda source: line_copy(node, z, source).wait_recv())
            for source in range(n_pcol):
                sum_at = sum_at + line_ref[source, blocks(node)]
            final_ref[blocks(node), piece_rows(z)] = sum_at
        else:
            others(add)
            final_ref[blocks(node), piece_rows(z)] = sum_ref[blocks(node), piece_rows(z)]

    def whole_copy(node, bit, start):
        part = rows(start, width // 2 ** (bit + 1))
        return pltpu.make_async_remote_copy(
            src_ref=final_ref.at[blocks(node), part],
            dst_ref=final_ref.at[blocks(node), part],
            send_sem=whole_send.at[node, bit],
            recv_sem=whole_recv.at[node, bit],
            device_id=partner(bit),
            device_id_type=MESH,
        )

    def whole_start(node, bit):
        whole_copy(node, bit, starts[bit + 1]).start()

    def whole_end(node, bit):
        whole_copy(node, bit, starts[bit + 1]).wait_recv()

    def write(node):
        for other in range(node + 1):
            block = final_ref[pair_at(other, node)]
            window_ref[other, node] = block
            if other < node:
                window_ref[node, other] = block.T

    def stage(node, at):
        if at == 0:
            g2_wait(node)
            multiply(node)
            rs_steps(node, False)
        elif at == 1:
            rs_steps(node, True)
        elif at == 2:
            rs_end(node)
            window_part(node)
            half_copy(node, 0).start()
        elif at < 3 + bits:
            bit = at - 3
            half_end(node, bit)
            if bit + 1 < bits:
                half_copy(node, bit + 1).start()
            else:
                others(lambda dest: line_copy(node, dest, z).start())
        elif at == 3 + bits:
            line_end(node)
            if not full:
                others(lambda dest: back_copy(node, dest, z).start())
        elif at == 4 + bits:
            if not full:
                others(lambda source: back_copy(node, z, source).wait_recv())
            whole_start(node, bits - 1)
        else:
            bit = 2 * bits + 4 - at
            whole_end(node, bit)
            if bit > 0:
                whole_start(node, bit - 1)
            else:
                write(node)

    loads[0].wait()
    loads[1].wait()
    local_v(order[0])
    pl.semaphore_wait(barrier, n_prow * n_pcol - 1)
    g1_start(order[0])
    loads[2].wait()
    for node in order[1:]:
        local_v(node)
        g1_start(node)
    loads[3].wait()
    a_split.append(split(a_ref[...]))
    for node in range(count):
        vt_split[node] = split(v_ref[node].T)
    g2_start(order[0])
    last = 5 + 2 * bits
    for turn in range(count + last - 1):
        if turn + 1 < count:
            g2_start(order[turn + 1])
        for at in range(last):
            if 0 <= turn - at < count:
                stage(order[turn - at], at)
    for node in order:
        g1_finish(node)
        g2_finish(node)
        rs_finish(node)
        for bit in range(bits):
            half_copy(node, bit).wait_send()
            whole_copy(node, bit, starts[bit + 1]).wait_send()
        others(lambda dest: line_copy(node, dest, z).wait_send())
        if not full:
            others(lambda dest: back_copy(node, dest, z).wait_send())


def sweep(n_prow, n_pcol, readers, anc_inverse, anc_factor, win_factor, diag_inverse):
    count, fine, width = anc_factor.shape
    pairs = count * (count + 1) // 2
    sources = n_prow // n_pcol * n_pcol
    share = count * width // (n_prow * n_pcol)
    bits = n_prow.bit_length() - 1
    region = width // n_prow
    piece = region if region // n_pcol % 8 != 0 else region // n_pcol
    vmem = pl.BlockSpec(memory_space=pltpu.VMEM)
    operands = (anc_inverse, anc_factor, win_factor, diag_inverse)
    return pl.pallas_call(
        functools.partial(kernel, n_prow, n_pcol),
        out_shape=(
            jax.ShapeDtypeStruct((count, fine, width), jnp.float32),
            jax.ShapeDtypeStruct((count, count, width, width), jnp.float32),
        ),
        in_specs=[pl.BlockSpec(memory_space=pltpu.SMEM)] + [pl.BlockSpec(memory_space=pltpu.HBM)] * 4,
        out_specs=(vmem, vmem),
        scratch_shapes=[pltpu.VMEM(operand.shape, jnp.float32) for operand in operands]
        + [
            pltpu.VMEM((count, fine + share, width), jnp.float32),
            pltpu.VMEM((count, sources, PIECES, fine // PIECES, width), jnp.float32),
            pltpu.VMEM((count, n_pcol, fine, width), jnp.float32),
            pltpu.VMEM((count, 2, n_pcol, fine, width), jnp.float32),
            pltpu.VMEM((pairs, width, width), jnp.float32),
            pltpu.VMEM((pairs, width, width), jnp.float32),
            pltpu.VMEM((n_pcol, pairs, piece, width), jnp.float32),
            pltpu.SemaphoreType.DMA((len(operands),)),
            pltpu.SemaphoreType.DMA((count, PIECES)),
            pltpu.SemaphoreType.DMA((count,)),
            pltpu.SemaphoreType.DMA((count, n_prow)),
            pltpu.SemaphoreType.DMA((count, PIECES)),
            pltpu.SemaphoreType.DMA((count, n_pcol)),
            pltpu.SemaphoreType.DMA((count, 2, n_pcol)),
            pltpu.SemaphoreType.DMA((count, bits)),
            pltpu.SemaphoreType.DMA((count, bits)),
            pltpu.SemaphoreType.DMA((count, n_pcol)),
            pltpu.SemaphoreType.DMA((count, n_pcol)),
            pltpu.SemaphoreType.DMA((count, n_pcol)),
            pltpu.SemaphoreType.DMA((count, n_pcol)),
            pltpu.SemaphoreType.DMA((count, bits)),
            pltpu.SemaphoreType.DMA((count, bits)),
        ]
        + [pltpu.VMEM((pairs, width // 2 ** (bit + 1), width), jnp.float32) for bit in range(bits)],
        compiler_params=pltpu.CompilerParams(
            collective_id=0, has_side_effects=True, vmem_limit_bytes=40 * 2**20
        ),
    )(readers, *operands)


def per_device(anc_inverse, anc_factor, win_factor, diag_inverse, first_reader):
    n_prow = lax.axis_size("prow")
    n_pcol = lax.axis_size("pcol")
    return sweep(n_prow, n_pcol, first_reader, anc_inverse, anc_factor, win_factor, diag_inverse)


def solution(mesh):
    return jax.shard_map(
        per_device,
        mesh=mesh,
        in_specs=(
            P(("groups", "prow"), "pcol"),
            P("groups", ("prow", "pcol"), None),
            P("groups", None, None),
            P("groups", None, None),
            P("groups"),
        ),
        out_specs=(P("groups", ("prow", "pcol"), None), P("groups", None, None, None)),
        check_vma=False,
    )
```
